32 devices in a mesh: section: 4 (over y, core), replica: 8 (over z, x).
Axes of the slice: x: 2, y: 2, z: 4, core: 2. Of those that a mesh axis runs over, the one named last changes fastest.
Arguments:
- tokens: bfloat16 [8, 128, 2048], P('replica', 'section'), may hold values from -6 to 6
- gate_weight: bfloat16 [4, 8, 2048, 384], P('section', 'replica'), may hold values from -0.125 to 0.125
- up_weight: bfloat16 [4, 8, 2048, 384], P('section', 'replica'), may hold values from -0.125 to 0.125
- slow_down: float32 [4, 8, 384, 2048], P('section', 'replica'), may hold values from -0.3125 to 0.3125
- prev_outer: bfloat16 [4, 8, 384, 2048], P('section', 'replica'), may hold values from -0.29882812 to 0.29882812
- route: int32 [3, 1, 8], replicated, may hold values from 0 to 7, each once within a row
- partner: int32 [8], replicated, may hold values from 0 to 7, as said below
Outputs:
- new_slow: float32 [4, 8, 384, 2048], P('section', 'replica')
- new_outer: bfloat16 [4, 8, 384, 2048], P('section', 'replica')
The draws below stay inside these ranges and needn't reach their ends.
Inputs may be any that keep to these rules, and one draw needn't show every extreme that they name: route[s, m] is a permutation of the replicas: replica r at section s hands micro-batch m to replica route[s, m, r] at section s + 1. partner pairs the replicas: partner[partner[r]] = r and partner[r] != r.
All inputs are finite; a program needn't handle non-finite values.
Results may differ from the reference program's by a relative error of at most 0.017.
Values may be sent and summed in bfloat16 or wider, within the bound.
No kernel may reach another device: no remote copies, remote signals or barrier semaphores. Data moves between devices by JAX's collectives and lax.ppermute only.
A program may use at most 128 MiB of HBM per device.

```python
import jax
import jax.numpy as jnp
from jax import lax

D = 2048
HID = 384
MT = 128
MB = 1
N_SECTION = 4
N_REPLICA = 8


def draw_partner(key, part):
    shuffled = jax.random.permutation(jax.random.fold_in(key, 7), N_REPLICA).astype(jnp.int32)
    paired = shuffled.reshape(-1, 2)
    result = jnp.zeros((N_REPLICA,), jnp.int32)
    result = result.at[paired[:, 0]].set(paired[:, 1])
    result = result.at[paired[:, 1]].set(paired[:, 0])
    return result


def shard_levels(stream_key, dims, pieces, low, top_value):
    loudness, own = 1.0, jax.random.fold_in(stream_key, 6)
    for dim, blocks in pieces:
        draws = jnp.exp(jax.random.uniform(jax.random.fold_in(own, dim), (blocks,), jnp.float32, low / len(pieces), top_value / len(pieces)))
        loudness = loudness * jnp.repeat(draws, dims[dim] // blocks).reshape([-1 if axis == dim else 1 for axis in range(len(dims))])
    return loudness


def gaussian(rng, extent, width, reach, split=(), kind=jnp.bfloat16):
    loudness = shard_levels(rng, extent, split, -0.22, 0.18) if split else 1.0
    array = jax.random.normal(rng, extent, jnp.float32) * width * loudness
    return jnp.minimum(jnp.maximum(array, -reach), reach).astype(kind)


def setup_inputs(seed: int = 0) -> dict:
    arg_keys = jax.random.split(jax.random.key(seed), 8)
    return {
        "tokens": gaussian(arg_keys[0], (N_REPLICA, MB * MT, D), 1.0, 6.0, ((0, 8), (1, 4))),
        "gate_weight": gaussian(arg_keys[1], (N_SECTION, N_REPLICA, D, HID), D ** -0.5, 0.125, ((0, 4), (1, 8))),
        "up_weight": gaussian(arg_keys[2], (N_SECTION, N_REPLICA, D, HID), D ** -0.5, 0.125, ((0, 4), (1, 8))),
        "slow_down": gaussian(arg_keys[3], (N_SECTION, N_REPLICA, HID, D), HID ** -0.5, 0.3125, ((0, 4), (1, 8)), jnp.float32),
        "prev_outer": gaussian(arg_keys[4], (N_SECTION, N_REPLICA, HID, D), 0.05, 0.29882812, ((0, 4), (1, 8))),
        "route": jax.vmap(lambda own: jax.random.permutation(own, N_REPLICA))(jax.random.split(arg_keys[5], (N_SECTION - 1) * MB)).reshape((N_SECTION - 1, MB, N_REPLICA)).astype(jnp.int32),
        "partner": draw_partner(jax.random.fold_in(arg_keys[7], 71), 0),
    }


EPSILON = 1e-05
OUTER_RATE = 0.7
MOMENTUM = 0.9

def section_forward(inputs, gate_w, up_w, down_w):
    widened = inputs.astype(jnp.float32)
    inv_rms = lax.rsqrt(lax.optimization_barrier(jnp.mean(widened * widened, axis=-1, keepdims=True)) + EPSILON)
    normed = (widened * inv_rms).astype(jnp.bfloat16)
    gate_act = jnp.dot(normed, gate_w, preferred_element_type=jnp.float32)
    up_act = jnp.dot(normed, up_w, preferred_element_type=jnp.float32)
    hidden = (jax.nn.silu(gate_act) * up_act).astype(jnp.bfloat16)
    output = (widened + jnp.dot(hidden, down_w, preferred_element_type=jnp.float32)).astype(jnp.bfloat16)
    return (output, gate_act, up_act, hidden)

def section_backward(inputs, gate_act, up_act, hidden, upstream, gate_w, up_w, down_w):
    contract_rows = (((0,), (0,)), ((), ()))
    contract_cols = (((1,), (1,)), ((), ()))
    grad_part = lax.dot_general(hidden, upstream, contract_rows, preferred_element_type=jnp.float32)
    hidden_grad = lax.dot_general(upstream, down_w, contract_cols, preferred_element_type=jnp.float32)
    sigmoid_gate = jax.nn.sigmoid(gate_act)
    gate_grad = (hidden_grad * up_act * sigmoid_gate * (1.0 + gate_act * (1.0 - sigmoid_gate))).astype(jnp.bfloat16)
    up_grad = (hidden_grad * gate_act * sigmoid_gate).astype(jnp.bfloat16)
    normed_grad = lax.dot_general(gate_grad, gate_w, contract_cols, preferred_element_type=jnp.float32)
    normed_grad = normed_grad + lax.dot_general(up_grad, up_w, contract_cols, preferred_element_type=jnp.float32)
    widened = inputs.astype(jnp.float32)
    inv_rms = lax.rsqrt(lax.optimization_barrier(jnp.mean(widened * widened, axis=-1, keepdims=True)) + EPSILON)
    input_grad = upstream.astype(jnp.float32) + inv_rms * normed_grad
    input_grad = input_grad - widened * inv_rms ** 3 * lax.optimization_barrier(jnp.mean(normed_grad * widened, axis=-1, keepdims=True))
    return (grad_part, input_grad.astype(jnp.bfloat16))

def reference(tokens, gate_weight, up_weight, slow_down, prev_outer, route, partner):
    current = tokens.reshape(N_REPLICA, MB, MT, D)
    saved = []
    produced = current
    for section_index in range(N_SECTION):
        down_fast = slow_down[section_index].astype(jnp.bfloat16)

        def run_forward(packed):
            rows, gate_w, up_w, down_w = packed
            output, gate_act, up_act, hidden = section_forward(rows.reshape(MB * MT, D), gate_w, up_w, down_w)
            return (output.reshape(MB, MT, D), gate_act, up_act, hidden)
        results = lax.map(run_forward, (current, gate_weight[section_index], up_weight[section_index], down_fast))
        saved.append((current, results[1], results[2], results[3], down_fast))
        produced = results[0]
        if section_index < N_SECTION - 1:
            routed = []
            for micro_index in range(MB):
                empty = jnp.zeros_like(produced[:, micro_index])
                routed.append(empty.at[route[section_index, micro_index]].set(produced[:, micro_index]))
            current = jnp.stack(routed, axis=1)
    upstream = (produced.astype(jnp.float32) / float(MB * MT)).astype(jnp.bfloat16)
    weight_grads = [None] * N_SECTION
    for section_index in range(N_SECTION - 1, -1, -1):
        inputs, gate_act, up_act, hidden, down_fast = saved[section_index]

        def run_backward(packed):
            rows, gate_a, up_a, hidden_a, upstream_a, gate_w, up_w, down_w = packed
            grad_part, input_grad = section_backward(rows.reshape(MB * MT, D), gate_a, up_a, hidden_a, upstream_a.reshape(MB * MT, D), gate_w, up_w, down_w)
            return (grad_part, input_grad.reshape(MB, MT, D))
        grad_part, input_grad = lax.map(run_backward, (inputs, gate_act, up_act, hidden, upstream, gate_weight[section_index], up_weight[section_index], down_fast))
        weight_grads[section_index] = grad_part
        if section_index > 0:
            upstream = jnp.stack([input_grad[route[section_index - 1, micro_index], micro_index] for micro_index in range(MB)], axis=1)
    weight_grad = jnp.stack(weight_grads)
    average_slow = 0.5 * (slow_down + slow_down[:, partner])
    average_prev = 0.5 * (prev_outer.astype(jnp.float32) + prev_outer[:, partner].astype(jnp.float32))
    velocity = MOMENTUM * average_prev + weight_grad
    new_slow = average_slow - OUTER_RATE * (weight_grad + MOMENTUM * velocity)
    return (new_slow, velocity.astype(jnp.bfloat16))
```

```python
import jax
import jax.numpy as jnp
from jax import lax
from jax.sharding import PartitionSpec as P

MT = 128
MB = 1


EPSILON = 1e-05
OUTER_RATE = 0.7
MOMENTUM = 0.9
DIRECT_SETS = 36
AXES = ("section", "replica")


def for_sending(shard):
    return jax.tree.map(lambda a: a.astype(jnp.bfloat16) if a.dtype == jnp.float32 else a, shard)


def passed_along(shard, axis, by):
    length = lax.axis_size(axis)
    pairs = [(i, i + by) for i in range(length) if 0 <= i + by < length]
    return lax.ppermute(shard, axis, pairs)


def section_forward(inputs, gate_w, up_w, down_w):
    widened = inputs.astype(jnp.float32)
    inv_rms = lax.rsqrt(jnp.mean(widened * widened, axis=-1, keepdims=True) + EPSILON)
    normed = (widened * inv_rms).astype(jnp.bfloat16)
    gate_act = jnp.dot(normed, gate_w, preferred_element_type=jnp.float32)
    up_act = jnp.dot(normed, up_w, preferred_element_type=jnp.float32)
    hidden = (jax.nn.silu(gate_act) * up_act).astype(jnp.bfloat16)
    output = (widened + jnp.dot(hidden, down_w, preferred_element_type=jnp.float32)).astype(
        jnp.bfloat16
    )
    return (output, gate_act, up_act, hidden)


def section_backward(inputs, gate_act, up_act, hidden, upstream, gate_w, up_w, down_w):
    contract_rows = (((0,), (0,)), ((), ()))
    contract_cols = (((1,), (1,)), ((), ()))
    grad_part = lax.dot_general(hidden, upstream, contract_rows, preferred_element_type=jnp.float32)
    hidden_grad = lax.dot_general(
        upstream, down_w, contract_cols, preferred_element_type=jnp.float32
    )
    sigmoid_gate = jax.nn.sigmoid(gate_act)
    gate_grad = (
        hidden_grad * up_act * sigmoid_gate * (1.0 + gate_act * (1.0 - sigmoid_gate))
    ).astype(jnp.bfloat16)
    up_grad = (hidden_grad * gate_act * sigmoid_gate).astype(jnp.bfloat16)
    normed_grad = lax.dot_general(
        gate_grad, gate_w, contract_cols, preferred_element_type=jnp.float32
    )
    normed_grad = normed_grad + lax.dot_general(
        up_grad, up_w, contract_cols, preferred_element_type=jnp.float32
    )
    widened = inputs.astype(jnp.float32)
    inv_rms = lax.rsqrt(jnp.mean(widened * widened, axis=-1, keepdims=True) + EPSILON)
    input_grad = upstream.astype(jnp.float32) + inv_rms * normed_grad
    input_grad = input_grad - widened * inv_rms**3 * jnp.mean(
        normed_grad * widened, axis=-1, keepdims=True
    )
    return (grad_part, input_grad.astype(jnp.bfloat16))


def permute_matrix(targets, replica_count):
    return (targets[None, :] == jnp.arange(replica_count, dtype=jnp.int32)[:, None]).astype(
        jnp.bfloat16
    )


def reorder(received, matrix):
    flat_rows = received.reshape(received.shape[0], -1)
    placed = jnp.dot(matrix, flat_rows, preferred_element_type=jnp.float32).astype(jnp.bfloat16)
    return placed.reshape(received.shape)


def route_block(act_block, matrix):
    return lax.all_to_all(
        reorder(
            lax.all_to_all(act_block[None], "replica", split_axis=2, concat_axis=0, tiled=True),
            matrix,
        ),
        "replica",
        split_axis=0,
        concat_axis=2,
        tiled=True,
    )[0]


def partner_copy(slow_weight, prior_outer, partner):
    received = (
        lax.all_to_all(
            slow_weight[None].astype(jnp.bfloat16),
            "replica",
            split_axis=1,
            concat_axis=0,
            tiled=True,
        ).astype(jnp.float32),
        lax.all_to_all(prior_outer[None], "replica", split_axis=1, concat_axis=0, tiled=True),
    )
    mates = lax.all_to_all(
        for_sending(tuple((jnp.take(member, partner, axis=0) for member in received))),
        "replica",
        split_axis=0,
        concat_axis=1,
        tiled=True,
    )
    return (mates[0][0], mates[1][0])


def store_slot(buffer, slot_index, is_live, new_value):
    previous = buffer[slot_index]
    return buffer.at[slot_index].set(jnp.where(is_live, new_value, previous))


def local_exchange(tokens, gate_weight, up_weight, slow_down, prev_outer, route, partner):
    section_count = lax.axis_size("section")
    replica_count = lax.axis_size("replica")
    section_id = lax.axis_index("section")
    gate_w = gate_weight[0, 0]
    up_w = up_weight[0, 0]
    slow_weight = slow_down[0, 0]
    prior_outer = prev_outer[0, 0]
    down_w = slow_weight.astype(jnp.bfloat16)
    feature_count = gate_w.shape[0]
    hidden_units = gate_w.shape[1]
    gathered = lax.all_gather(tokens[0], "section", axis=0, tiled=True).reshape(
        MB, MT, feature_count
    )
    turn_count = MB + section_count - 1
    saved_in = jnp.zeros((MB, MT, feature_count), jnp.bfloat16)
    saved_out = jnp.zeros((MB, MT, feature_count), jnp.bfloat16)
    saved_gate = jnp.zeros((MB, MT, hidden_units), jnp.float32)
    saved_up = jnp.zeros((MB, MT, hidden_units), jnp.float32)
    saved_hidden = jnp.zeros((MB, MT, hidden_units), jnp.bfloat16)
    arriving = jnp.zeros((MT, feature_count), jnp.bfloat16)
    for turn_index in range(turn_count):
        micro_batch = turn_index - section_id
        is_live = (micro_batch >= 0) & (micro_batch < MB)
        slot_index = jnp.clip(micro_batch, 0, MB - 1)
        fresh_rows = gathered[min(turn_index, MB - 1)]
        inputs = jnp.where(section_id == 0, fresh_rows, arriving)
        output, gate_act, up_act, hidden = section_forward(inputs, gate_w, up_w, down_w)
        saved_in = store_slot(saved_in, slot_index, is_live, inputs)
        saved_out = store_slot(saved_out, slot_index, is_live, output)
        saved_gate = store_slot(saved_gate, slot_index, is_live, gate_act)
        saved_up = store_slot(saved_up, slot_index, is_live, up_act)
        saved_hidden = store_slot(saved_hidden, slot_index, is_live, hidden)
        if turn_index < turn_count - 1:
            boundary = jnp.minimum(section_id, section_count - 2)
            matrix = permute_matrix(route[boundary, slot_index], replica_count)
            arriving = passed_along(route_block(output, matrix), "section", 1)
    weight_grad = jnp.zeros((hidden_units, feature_count), jnp.float32)
    arriving = jnp.zeros((MT, feature_count), jnp.bfloat16)
    for turn_index in range(turn_count):
        micro_batch = turn_index - (section_count - 1 - section_id)
        is_live = (micro_batch >= 0) & (micro_batch < MB)
        slot_index = jnp.clip(micro_batch, 0, MB - 1)
        loss_grad = (saved_out[slot_index].astype(jnp.float32) / float(MB * MT)).astype(
            jnp.bfloat16
        )
        upstream = jnp.where(section_id == section_count - 1, loss_grad, arriving)
        grad_part, input_grad = section_backward(
            saved_in[slot_index],
            saved_gate[slot_index],
            saved_up[slot_index],
            saved_hidden[slot_index],
            upstream,
            gate_w,
            up_w,
            down_w,
        )
        weight_grad = weight_grad + jnp.where(is_live, grad_part, 0.0)
        if turn_index < turn_count - 1:
            boundary = jnp.maximum(section_id - 1, 0)
            matrix = permute_matrix(route[boundary, slot_index], replica_count).T
            arriving = passed_along(route_block(input_grad, matrix), "section", -1)
    mate_slow, mate_prior = partner_copy(slow_weight, prior_outer, partner)
    average_slow = 0.5 * (slow_weight + mate_slow)
    average_prev = 0.5 * (prior_outer.astype(jnp.float32) + mate_prior.astype(jnp.float32))
    velocity = MOMENTUM * average_prev + weight_grad
    new_slow = average_slow - OUTER_RATE * (weight_grad + MOMENTUM * velocity)
    return (new_slow[None, None], velocity.astype(jnp.bfloat16)[None, None])


def reflected(k, i, length):
    return (k - i) % length


def hop_pairs(parity, k, section_count, replica_count, way):
    pairs = []
    for h in range(parity, section_count - 1, 2):
        for i in range(replica_count):
            low = h * replica_count + i
            high = (h + 1) * replica_count + reflected(k, i, replica_count)
            if way >= 0:
                pairs.append((low, high))
            if way <= 0:
                pairs.append((high, low))
    return pairs


def mate_pairs(k, section_count, replica_count):
    return [
        (s * replica_count + i, s * replica_count + reflected(k, i, replica_count))
        for s in range(section_count)
        for i in range(replica_count)
        if reflected(k, i, replica_count) != i
    ]


def choose_transfer(value, choice, pair_sets):
    branches = [lambda v, pairs=pairs: lax.ppermute(v, AXES, pairs) for pairs in pair_sets]
    branches.append(lambda v: v)
    return lax.switch(choice, branches, value)


def local_direct(tokens, gate_weight, up_weight, slow_down, prev_outer, route, partner):
    section_count = lax.axis_size("section")
    replica_count = lax.axis_size("replica")
    section_id = lax.axis_index("section")
    replica_id = lax.axis_index("replica")
    gate_w = gate_weight[0, 0]
    up_w = up_weight[0, 0]
    slow_weight = slow_down[0, 0]
    prior_outer = prev_outer[0, 0]
    down_w = slow_weight.astype(jnp.bfloat16)
    idle = jnp.int32(replica_count)

    table = jnp.concatenate([route[:, 0], partner[None]], axis=0)
    lanes = jnp.arange(replica_count, dtype=jnp.int32)[None]
    row = jnp.arange(section_count, dtype=jnp.int32)
    onward = jnp.sum(jnp.where(lanes == replica_id, table, 0), axis=1)
    origin = jnp.sum(jnp.where(table == replica_id, lanes, 0), axis=1)
    other = jnp.where(row + 1 == section_id, origin, onward) + replica_id
    classes = jnp.where(other >= replica_count, other - replica_count, other)
    taking_part = (row == section_id) | (row + 1 == section_id) | (row == section_count - 1)
    hop_class = jnp.where(taking_part, classes, idle)
    mate_class = classes[section_count - 1]

    counts = (section_count, replica_count)
    def hop(value, h, way):
        ways = 0 if h % 2 else way
        sets = [hop_pairs(h % 2, k, *counts, ways) for k in range(replica_count)]
        choice = hop_class[h]
        if h == section_count - 1:
            choice = idle
        return choose_transfer(value, choice, sets)

    mate_sets = [mate_pairs(k, *counts) for k in range(replica_count)]

    def mate(value, sections):
        here = section_id == sections[0]
        for s in sections[1:]:
            here = here | (section_id == s)
        return choose_transfer(value, jnp.where(here, mate_class, idle), mate_sets)

    pieces = [tokens[0]]
    for s in range(1, section_count):
        pairs = [(s * replica_count + i, i) for i in range(replica_count)]
        pieces.append(lax.ppermute(tokens[0], AXES, pairs))
    inputs = jnp.concatenate(pieces, axis=0)

    last = section_count - 1
    sent_slow = down_w
    saved = []
    mates = {}
    for t in range(section_count):
        output, gate_act, up_act, hidden = section_forward(inputs, gate_w, up_w, down_w)
        saved.append((inputs, gate_act, up_act, hidden))
        if t < last:
            inputs = hop(output, t, 1)
        if t == 0:
            early = [0, *range(2, section_count)]
            mates["slow_early"] = mate(sent_slow, early)
            mates["prior_early"] = mate(prior_outer, [0])
        if t == 1:
            mates["slow_late"] = mate(sent_slow, [1])
            mates["prior_mid"] = mate(prior_outer, [1])
    upstream = (output.astype(jnp.float32) / float(MB * MT)).astype(jnp.bfloat16)
    chosen_hidden, chosen_upstream = saved[last][3], upstream
    for t in range(last, 0, -1):
        _, input_grad = section_backward(*saved[t], upstream, gate_w, up_w, down_w)
        upstream = hop(input_grad, t - 1, -1)
        if t == 2:
            mates["prior_late"] = mate(prior_outer, list(range(2, section_count)))
        chosen_hidden = jnp.where(section_id == t - 1, saved[t - 1][3], chosen_hidden)
        chosen_upstream = jnp.where(section_id == t - 1, upstream, chosen_upstream)
    weight_grad = lax.dot_general(
        chosen_hidden, chosen_upstream, (((0,), (0,)), ((), ())), preferred_element_type=jnp.float32
    )
    second = section_id == 1
    mate_slow = jnp.where(second, mates["slow_late"], mates["slow_early"])
    mate_prior = jnp.where(
        second,
        mates["prior_mid"],
        jnp.where(section_id == 0, mates["prior_early"], mates["prior_late"]),
    )
    average_slow = 0.5 * (slow_weight + mate_slow.astype(jnp.float32))
    average_prev = 0.5 * (prior_outer.astype(jnp.float32) + mate_prior.astype(jnp.float32))
    velocity = MOMENTUM * average_prev + weight_grad
    new_slow = average_slow - OUTER_RATE * (weight_grad + MOMENTUM * velocity)
    return (new_slow[None, None], velocity.astype(jnp.bfloat16)[None, None])


def solution(mesh):
    pair_sets = 4 * mesh.shape["replica"] + mesh.shape["section"] - 1
    local = local_direct if pair_sets <= DIRECT_SETS else local_exchange
    placed = (
        P("replica", "section", None),
        P("section", "replica", None, None),
        P("section", "replica", None, None),
        P("section", "replica", None, None),
        P("section", "replica", None, None),
        P(),
        P(),
    )
    return jax.shard_map(
        local,
        mesh=mesh,
        in_specs=placed,
        out_specs=(P("section", "replica", None, None), P("section", "replica", None, None)),
        check_vma=False,
    )
```

```python
import jax
import jax.numpy as jnp
from jax import lax
from jax.sharding import PartitionSpec as P

MT = 128
MB = 1


EPSILON = 1e-05
OUTER_RATE = 0.7
MOMENTUM = 0.9
DIRECT_SETS = 36
AXES = ("section", "replica")
MATE_ROWS = 128
GOSSIP_PLAN = ((0, 1, 2, 4), (6, 0, 0, 0), (0, 5, 0, 0), (6, 6, 6, 6))


def for_sending(shard):
    return jax.tree.map(lambda a: a.astype(jnp.bfloat16) if a.dtype == jnp.float32 else a, shard)


def passed_along(shard, axis, by):
    length = lax.axis_size(axis)
    pairs = [(i, i + by) for i in range(length) if 0 <= i + by < length]
    return lax.ppermute(shard, axis, pairs)


def section_forward(inputs, gate_w, up_w, down_w):
    widened = inputs.astype(jnp.float32)
    inv_rms = lax.rsqrt(jnp.mean(widened * widened, axis=-1, keepdims=True) + EPSILON)
    normed = (widened * inv_rms).astype(jnp.bfloat16)
    gate_act = jnp.dot(normed, gate_w, preferred_element_type=jnp.float32)
    up_act = jnp.dot(normed, up_w, preferred_element_type=jnp.float32)
    hidden = (jax.nn.silu(gate_act) * up_act).astype(jnp.bfloat16)
    output = (widened + jnp.dot(hidden, down_w, preferred_element_type=jnp.float32)).astype(
        jnp.bfloat16
    )
    return (output, gate_act, up_act, hidden)


def section_backward(inputs, gate_act, up_act, hidden, upstream, gate_w, up_w, down_w):
    contract_rows = (((0,), (0,)), ((), ()))
    contract_cols = (((1,), (1,)), ((), ()))
    grad_part = lax.dot_general(hidden, upstream, contract_rows, preferred_element_type=jnp.float32)
    hidden_grad = lax.dot_general(
        upstream, down_w, contract_cols, preferred_element_type=jnp.float32
    )
    sigmoid_gate = jax.nn.sigmoid(gate_act)
    gate_grad = (
        hidden_grad * up_act * sigmoid_gate * (1.0 + gate_act * (1.0 - sigmoid_gate))
    ).astype(jnp.bfloat16)
    up_grad = (hidden_grad * gate_act * sigmoid_gate).astype(jnp.bfloat16)
    normed_grad = lax.dot_general(
        gate_grad, gate_w, contract_cols, preferred_element_type=jnp.float32
    )
    normed_grad = normed_grad + lax.dot_general(
        up_grad, up_w, contract_cols, preferred_element_type=jnp.float32
    )
    widened = inputs.astype(jnp.float32)
    inv_rms = lax.rsqrt(jnp.mean(widened * widened, axis=-1, keepdims=True) + EPSILON)
    input_grad = upstream.astype(jnp.float32) + inv_rms * normed_grad
    input_grad = input_grad - widened * inv_rms**3 * jnp.mean(
        normed_grad * widened, axis=-1, keepdims=True
    )
    return (grad_part, input_grad.astype(jnp.bfloat16))


def permute_matrix(targets, replica_count):
    return (targets[None, :] == jnp.arange(replica_count, dtype=jnp.int32)[:, None]).astype(
        jnp.bfloat16
    )


def reorder(received, matrix):
    flat_rows = received.reshape(received.shape[0], -1)
    placed = jnp.dot(matrix, flat_rows, preferred_element_type=jnp.float32).astype(jnp.bfloat16)
    return placed.reshape(received.shape)


def route_block(act_block, matrix):
    return lax.all_to_all(
        reorder(
            lax.all_to_all(act_block[None], "replica", split_axis=2, concat_axis=0, tiled=True),
            matrix,
        ),
        "replica",
        split_axis=0,
        concat_axis=2,
        tiled=True,
    )[0]


def partner_copy(slow_weight, prior_outer, partner):
    received = (
        lax.all_to_all(
            slow_weight[None].astype(jnp.bfloat16),
            "replica",
            split_axis=1,
            concat_axis=0,
            tiled=True,
        ).astype(jnp.float32),
        lax.all_to_all(prior_outer[None], "replica", split_axis=1, concat_axis=0, tiled=True),
    )
    mates = lax.all_to_all(
        for_sending(tuple((jnp.take(member, partner, axis=0) for member in received))),
        "replica",
        split_axis=0,
        concat_axis=1,
        tiled=True,
    )
    return (mates[0][0], mates[1][0])


def store_slot(buffer, slot_index, is_live, new_value):
    previous = buffer[slot_index]
    return buffer.at[slot_index].set(jnp.where(is_live, new_value, previous))


def local_exchange(tokens, gate_weight, up_weight, slow_down, prev_outer, route, partner):
    section_count = lax.axis_size("section")
    replica_count = lax.axis_size("replica")
    section_id = lax.axis_index("section")
    gate_w = gate_weight[0, 0]
    up_w = up_weight[0, 0]
    slow_weight = slow_down[0, 0]
    prior_outer = prev_outer[0, 0]
    down_w = slow_weight.astype(jnp.bfloat16)
    feature_count = gate_w.shape[0]
    hidden_units = gate_w.shape[1]
    gathered = lax.all_gather(tokens[0], "section", axis=0, tiled=True).reshape(
        MB, MT, feature_count
    )
    turn_count = MB + section_count - 1
    saved_in = jnp.zeros((MB, MT, feature_count), jnp.bfloat16)
    saved_out = jnp.zeros((MB, MT, feature_count), jnp.bfloat16)
    saved_gate = jnp.zeros((MB, MT, hidden_units), jnp.float32)
    saved_up = jnp.zeros((MB, MT, hidden_units), jnp.float32)
    saved_hidden = jnp.zeros((MB, MT, hidden_units), jnp.bfloat16)
    arriving = jnp.zeros((MT, feature_count), jnp.bfloat16)
    for turn_index in range(turn_count):
        micro_batch = turn_index - section_id
        is_live = (micro_batch >= 0) & (micro_batch < MB)
        slot_index = jnp.clip(micro_batch, 0, MB - 1)
        fresh_rows = gathered[min(turn_index, MB - 1)]
        inputs = jnp.where(section_id == 0, fresh_rows, arriving)
        output, gate_act, up_act, hidden = section_forward(inputs, gate_w, up_w, down_w)
        saved_in = store_slot(saved_in, slot_index, is_live, inputs)
        saved_out = store_slot(saved_out, slot_index, is_live, output)
        saved_gate = store_slot(saved_gate, slot_index, is_live, gate_act)
        saved_up = store_slot(saved_up, slot_index, is_live, up_act)
        saved_hidden = store_slot(saved_hidden, slot_index, is_live, hidden)
        if turn_index < turn_count - 1:
            boundary = jnp.minimum(section_id, section_count - 2)
            matrix = permute_matrix(route[boundary, slot_index], replica_count)
            arriving = passed_along(route_block(output, matrix), "section", 1)
    weight_grad = jnp.zeros((hidden_units, feature_count), jnp.float32)
    arriving = jnp.zeros((MT, feature_count), jnp.bfloat16)
    for turn_index in range(turn_count):
        micro_batch = turn_index - (section_count - 1 - section_id)
        is_live = (micro_batch >= 0) & (micro_batch < MB)
        slot_index = jnp.clip(micro_batch, 0, MB - 1)
        loss_grad = (saved_out[slot_index].astype(jnp.float32) / float(MB * MT)).astype(
            jnp.bfloat16
        )
        upstream = jnp.where(section_id == section_count - 1, loss_grad, arriving)
        grad_part, input_grad = section_backward(
            saved_in[slot_index],
            saved_gate[slot_index],
            saved_up[slot_index],
            saved_hidden[slot_index],
            upstream,
            gate_w,
            up_w,
            down_w,
        )
        weight_grad = weight_grad + jnp.where(is_live, grad_part, 0.0)
        if turn_index < turn_count - 1:
            boundary = jnp.maximum(section_id - 1, 0)
            matrix = permute_matrix(route[boundary, slot_index], replica_count).T
            arriving = passed_along(route_block(input_grad, matrix), "section", -1)
    mate_slow, mate_prior = partner_copy(slow_weight, prior_outer, partner)
    average_slow = 0.5 * (slow_weight + mate_slow)
    average_prev = 0.5 * (prior_outer.astype(jnp.float32) + mate_prior.astype(jnp.float32))
    velocity = MOMENTUM * average_prev + weight_grad
    new_slow = average_slow - OUTER_RATE * (weight_grad + MOMENTUM * velocity)
    return (new_slow[None, None], velocity.astype(jnp.bfloat16)[None, None])


def reflected(k, i, length):
    return (k - i) % length


def hop_pairs(parity, k, section_count, replica_count, way):
    pairs = []
    for h in range(parity, section_count - 1, 2):
        for i in range(replica_count):
            low = h * replica_count + i
            high = (h + 1) * replica_count + reflected(k, i, replica_count)
            if way >= 0:
                pairs.append((low, high))
            if way <= 0:
                pairs.append((high, low))
    return pairs


def mate_pairs(k, section_count, replica_count):
    return [
        (s * replica_count + i, s * replica_count + reflected(k, i, replica_count))
        for s in range(section_count)
        for i in range(replica_count)
        if reflected(k, i, replica_count) != i
    ]


def choose_transfer(value, choice, pair_sets):
    branches = [lambda v, pairs=pairs: lax.ppermute(v, AXES, pairs) for pairs in pair_sets]
    branches.append(lambda v: v)
    return lax.switch(choice, branches, value)


def local_direct(tokens, gate_weight, up_weight, slow_down, prev_outer, route, partner):
    section_count = lax.axis_size("section")
    replica_count = lax.axis_size("replica")
    section_id = lax.axis_index("section")
    replica_id = lax.axis_index("replica")
    gate_w = gate_weight[0, 0]
    up_w = up_weight[0, 0]
    slow_weight = slow_down[0, 0]
    prior_outer = prev_outer[0, 0]
    down_w = slow_weight.astype(jnp.bfloat16)
    idle = jnp.int32(replica_count)

    table = jnp.concatenate([route[:, 0], partner[None]], axis=0)
    lanes = jnp.arange(replica_count, dtype=jnp.int32)[None]
    row = jnp.arange(section_count, dtype=jnp.int32)
    onward = jnp.sum(jnp.where(lanes == replica_id, table, 0), axis=1)
    origin = jnp.sum(jnp.where(table == replica_id, lanes, 0), axis=1)
    other = jnp.where(row + 1 == section_id, origin, onward) + replica_id
    classes = jnp.where(other >= replica_count, other - replica_count, other)
    taking_part = (row == section_id) | (row + 1 == section_id) | (row == section_count - 1)
    choices = jnp.where(taking_part, classes, idle)

    counts = (section_count, replica_count)

    def hop(value, h, way):
        ways = 0 if h % 2 else way
        sets = [hop_pairs(h % 2, k, *counts, ways) for k in range(replica_count)]
        return choose_transfer(value, choices[h], sets)

    mate_sets = [mate_pairs(k, *counts) for k in range(replica_count)]
    unit = min(MATE_ROWS, slow_weight.shape[0])
    units = 2 * slow_weight.shape[0] // unit

    def by_section(values):
        result = jnp.int32(values[-1])
        for s in range(section_count - 1):
            result = jnp.where(section_id == s, jnp.int32(values[s]), result)
        return result

    done_units = [0] * section_count

    def gossip(buffer, amounts):
        begin = list(done_units)
        for s in range(section_count):
            done_units[s] = min(units, done_units[s] + amounts[s])

        def step(index, held):
            piece = lax.dynamic_slice_in_dim(held, index * unit, unit, axis=0)
            piece = choose_transfer(piece, choices[section_count - 1], mate_sets)
            return lax.dynamic_update_slice_in_dim(held, piece, index * unit, axis=0)

        return lax.fori_loop(by_section(begin), by_section(done_units), step, buffer)

    plan = GOSSIP_PLAN if section_count == len(GOSSIP_PLAN[0]) else []
    buffer = jnp.concatenate([down_w, prior_outer], axis=0)

    pieces = [tokens[0]]
    for s in range(1, section_count):
        pairs = [(s * replica_count + i, i) for i in range(replica_count)]
        pieces.append(lax.ppermute(tokens[0], AXES, pairs))
    inputs = jnp.concatenate(pieces, axis=0)

    last = section_count - 1
    saved = []
    point = 0
    for t in range(section_count):
        output, gate_act, up_act, hidden = section_forward(inputs, gate_w, up_w, down_w)
        saved.append((inputs, gate_act, up_act, hidden))
        if t < last:
            if plan:
                buffer = gossip(buffer, plan[point])
            point += 1
            output, buffer = lax.optimization_barrier((output, buffer))
            inputs = hop(output, t, 1)
            inputs, buffer = lax.optimization_barrier((inputs, buffer))
    upstream = (output.astype(jnp.float32) / float(MB * MT)).astype(jnp.bfloat16)
    chosen_hidden, chosen_upstream = saved[last][3], upstream
    for t in range(last, 0, -1):
        _, input_grad = section_backward(*saved[t], upstream, gate_w, up_w, down_w)
        if t == 1:
            amounts = plan[point] if plan else [units] * section_count
            buffer = gossip(buffer, amounts)
        input_grad, buffer = lax.optimization_barrier((input_grad, buffer))
        upstream = hop(input_grad, t - 1, -1)
        upstream, buffer = lax.optimization_barrier((upstream, buffer))
        chosen_hidden = jnp.where(section_id == t - 1, saved[t - 1][3], chosen_hidden)
        chosen_upstream = jnp.where(section_id == t - 1, upstream, chosen_upstream)
    weight_grad = lax.dot_general(
        chosen_hidden, chosen_upstream, (((0,), (0,)), ((), ())), preferred_element_type=jnp.float32
    )
    half = slow_weight.shape[0]
    average_slow = 0.5 * (slow_weight + buffer[:half].astype(jnp.float32))
    average_prev = 0.5 * (prior_outer.astype(jnp.float32) + buffer[half:].astype(jnp.float32))
    velocity = MOMENTUM * average_prev + weight_grad
    new_slow = average_slow - OUTER_RATE * (weight_grad + MOMENTUM * velocity)
    return (new_slow[None, None], velocity.astype(jnp.bfloat16)[None, None])


def solution(mesh):
    pair_sets = 4 * mesh.shape["replica"] + mesh.shape["section"] - 1
    local = local_direct if pair_sets <= DIRECT_SETS else local_exchange
    placed = (
        P("replica", "section", None),
        P("section", "replica", None, None),
        P("section", "replica", None, None),
        P("section", "replica", None, None),
        P("section", "replica", None, None),
        P(),
        P(),
    )
    return jax.shard_map(
        local,
        mesh=mesh,
        in_specs=placed,
        out_specs=(P("section", "replica", None, None), P("section", "replica", None, None)),
        check_vma=False,
    )
```

```python
import jax
import jax.numpy as jnp
from jax import lax
from jax.sharding import PartitionSpec as P

MT = 128
MB = 1


EPSILON = 1e-05
OUTER_RATE = 0.7
MOMENTUM = 0.9
DIRECT_SETS = 36
AXES = ("section", "replica")
DIRECT_SECTIONS = 4


def for_sending(shard):
    return jax.tree.map(lambda a: a.astype(jnp.bfloat16) if a.dtype == jnp.float32 else a, shard)


def passed_along(shard, axis, by):
    length = lax.axis_size(axis)
    pairs = [(i, i + by) for i in range(length) if 0 <= i + by < length]
    return lax.ppermute(shard, axis, pairs)


def section_forward(inputs, gate_w, up_w, down_w):
    widened = inputs.astype(jnp.float32)
    inv_rms = lax.rsqrt(jnp.mean(widened * widened, axis=-1, keepdims=True) + EPSILON)
    normed = (widened * inv_rms).astype(jnp.bfloat16)
    gate_act = jnp.dot(normed, gate_w, preferred_element_type=jnp.float32)
    up_act = jnp.dot(normed, up_w, preferred_element_type=jnp.float32)
    hidden = (jax.nn.silu(gate_act) * up_act).astype(jnp.bfloat16)
    output = (widened + jnp.dot(hidden, down_w, preferred_element_type=jnp.float32)).astype(
        jnp.bfloat16
    )
    return (output, gate_act, up_act, hidden)


def section_backward(inputs, gate_act, up_act, hidden, upstream, gate_w, up_w, down_w):
    contract_rows = (((0,), (0,)), ((), ()))
    contract_cols = (((1,), (1,)), ((), ()))
    grad_part = lax.dot_general(hidden, upstream, contract_rows, preferred_element_type=jnp.float32)
    hidden_grad = lax.dot_general(
        upstream, down_w, contract_cols, preferred_element_type=jnp.float32
    )
    sigmoid_gate = jax.nn.sigmoid(gate_act)
    gate_grad = (
        hidden_grad * up_act * sigmoid_gate * (1.0 + gate_act * (1.0 - sigmoid_gate))
    ).astype(jnp.bfloat16)
    up_grad = (hidden_grad * gate_act * sigmoid_gate).astype(jnp.bfloat16)
    normed_grad = lax.dot_general(
        gate_grad, gate_w, contract_cols, preferred_element_type=jnp.float32
    )
    normed_grad = normed_grad + lax.dot_general(
        up_grad, up_w, contract_cols, preferred_element_type=jnp.float32
    )
    widened = inputs.astype(jnp.float32)
    inv_rms = lax.rsqrt(jnp.mean(widened * widened, axis=-1, keepdims=True) + EPSILON)
    input_grad = upstream.astype(jnp.float32) + inv_rms * normed_grad
    input_grad = input_grad - widened * inv_rms**3 * jnp.mean(
        normed_grad * widened, axis=-1, keepdims=True
    )
    return (grad_part, input_grad.astype(jnp.bfloat16))


def permute_matrix(targets, replica_count):
    return (targets[None, :] == jnp.arange(replica_count, dtype=jnp.int32)[:, None]).astype(
        jnp.bfloat16
    )


def reorder(received, matrix):
    flat_rows = received.reshape(received.shape[0], -1)
    placed = jnp.dot(matrix, flat_rows, preferred_element_type=jnp.float32).astype(jnp.bfloat16)
    return placed.reshape(received.shape)


def route_block(act_block, matrix):
    return lax.all_to_all(
        reorder(
            lax.all_to_all(act_block[None], "replica", split_axis=2, concat_axis=0, tiled=True),
            matrix,
        ),
        "replica",
        split_axis=0,
        concat_axis=2,
        tiled=True,
    )[0]


def partner_copy(slow_weight, prior_outer, partner):
    received = (
        lax.all_to_all(
            slow_weight[None].astype(jnp.bfloat16),
            "replica",
            split_axis=1,
            concat_axis=0,
            tiled=True,
        ).astype(jnp.float32),
        lax.all_to_all(prior_outer[None], "replica", split_axis=1, concat_axis=0, tiled=True),
    )
    mates = lax.all_to_all(
        for_sending(tuple((jnp.take(member, partner, axis=0) for member in received))),
        "replica",
        split_axis=0,
        concat_axis=1,
        tiled=True,
    )
    return (mates[0][0], mates[1][0])


def store_slot(buffer, slot_index, is_live, new_value):
    previous = buffer[slot_index]
    return buffer.at[slot_index].set(jnp.where(is_live, new_value, previous))


def local_exchange(tokens, gate_weight, up_weight, slow_down, prev_outer, route, partner):
    section_count = lax.axis_size("section")
    replica_count = lax.axis_size("replica")
    section_id = lax.axis_index("section")
    gate_w = gate_weight[0, 0]
    up_w = up_weight[0, 0]
    slow_weight = slow_down[0, 0]
    prior_outer = prev_outer[0, 0]
    down_w = slow_weight.astype(jnp.bfloat16)
    feature_count = gate_w.shape[0]
    hidden_units = gate_w.shape[1]
    gathered = lax.all_gather(tokens[0], "section", axis=0, tiled=True).reshape(
        MB, MT, feature_count
    )
    turn_count = MB + section_count - 1
    saved_in = jnp.zeros((MB, MT, feature_count), jnp.bfloat16)
    saved_out = jnp.zeros((MB, MT, feature_count), jnp.bfloat16)
    saved_gate = jnp.zeros((MB, MT, hidden_units), jnp.float32)
    saved_up = jnp.zeros((MB, MT, hidden_units), jnp.float32)
    saved_hidden = jnp.zeros((MB, MT, hidden_units), jnp.bfloat16)
    arriving = jnp.zeros((MT, feature_count), jnp.bfloat16)
    for turn_index in range(turn_count):
        micro_batch = turn_index - section_id
        is_live = (micro_batch >= 0) & (micro_batch < MB)
        slot_index = jnp.clip(micro_batch, 0, MB - 1)
        fresh_rows = gathered[min(turn_index, MB - 1)]
        inputs = jnp.where(section_id == 0, fresh_rows, arriving)
        output, gate_act, up_act, hidden = section_forward(inputs, gate_w, up_w, down_w)
        saved_in = store_slot(saved_in, slot_index, is_live, inputs)
        saved_out = store_slot(saved_out, slot_index, is_live, output)
        saved_gate = store_slot(saved_gate, slot_index, is_live, gate_act)
        saved_up = store_slot(saved_up, slot_index, is_live, up_act)
        saved_hidden = store_slot(saved_hidden, slot_index, is_live, hidden)
        if turn_index < turn_count - 1:
            boundary = jnp.minimum(section_id, section_count - 2)
            matrix = permute_matrix(route[boundary, slot_index], replica_count)
            arriving = passed_along(route_block(output, matrix), "section", 1)
    weight_grad = jnp.zeros((hidden_units, feature_count), jnp.float32)
    arriving = jnp.zeros((MT, feature_count), jnp.bfloat16)
    for turn_index in range(turn_count):
        micro_batch = turn_index - (section_count - 1 - section_id)
        is_live = (micro_batch >= 0) & (micro_batch < MB)
        slot_index = jnp.clip(micro_batch, 0, MB - 1)
        loss_grad = (saved_out[slot_index].astype(jnp.float32) / float(MB * MT)).astype(
            jnp.bfloat16
        )
        upstream = jnp.where(section_id == section_count - 1, loss_grad, arriving)
        grad_part, input_grad = section_backward(
            saved_in[slot_index],
            saved_gate[slot_index],
            saved_up[slot_index],
            saved_hidden[slot_index],
            upstream,
            gate_w,
            up_w,
            down_w,
        )
        weight_grad = weight_grad + jnp.where(is_live, grad_part, 0.0)
        if turn_index < turn_count - 1:
            boundary = jnp.maximum(section_id - 1, 0)
            matrix = permute_matrix(route[boundary, slot_index], replica_count).T
            arriving = passed_along(route_block(input_grad, matrix), "section", -1)
    mate_slow, mate_prior = partner_copy(slow_weight, prior_outer, partner)
    average_slow = 0.5 * (slow_weight + mate_slow)
    average_prev = 0.5 * (prior_outer.astype(jnp.float32) + mate_prior.astype(jnp.float32))
    velocity = MOMENTUM * average_prev + weight_grad
    new_slow = average_slow - OUTER_RATE * (weight_grad + MOMENTUM * velocity)
    return (new_slow[None, None], velocity.astype(jnp.bfloat16)[None, None])


def reflected(k, i, length):
    return (k - i) % length


def hop_pairs(parity, k, section_count, replica_count, way):
    pairs = []
    for h in range(parity, section_count - 1, 2):
        for i in range(replica_count):
            low = h * replica_count + i
            high = (h + 1) * replica_count + reflected(k, i, replica_count)
            if way >= 0:
                pairs.append((low, high))
            if way <= 0:
                pairs.append((high, low))
    return pairs


def mate_pairs(k, section_count, replica_count):
    return [
        (s * replica_count + i, s * replica_count + (i ^ k))
        for s in range(section_count)
        for i in range(replica_count)
    ]


def choose_transfer(value, choice, pair_sets):
    branches = [lambda v, pairs=pairs: lax.ppermute(v, AXES, pairs) for pairs in pair_sets]
    branches.append(lambda v: v)
    return lax.switch(choice, branches, value)


def joint_forward(inputs, wide_w, down_w):
    hidden_units = wide_w.shape[1] // 2
    widened = inputs.astype(jnp.float32)
    inv_rms = lax.rsqrt(jnp.mean(widened * widened, axis=-1, keepdims=True) + EPSILON)
    normed = (widened * inv_rms).astype(jnp.bfloat16)
    acts = jnp.dot(normed, wide_w, preferred_element_type=jnp.float32)
    gate_act, up_act = acts[:, :hidden_units], acts[:, hidden_units:]
    hidden = (jax.nn.silu(gate_act) * up_act).astype(jnp.bfloat16)
    output = (widened + jnp.dot(hidden, down_w, preferred_element_type=jnp.float32)).astype(
        jnp.bfloat16
    )
    return output, acts, hidden


def joint_backward(inputs, acts, upstream, wide_w, down_w):
    contract_cols = (((1,), (1,)), ((), ()))
    hidden_units = wide_w.shape[1] // 2
    gate_act, up_act = acts[:, :hidden_units], acts[:, hidden_units:]
    hidden_grad = lax.dot_general(
        upstream, down_w, contract_cols, preferred_element_type=jnp.float32
    )
    sigmoid_gate = jax.nn.sigmoid(gate_act)
    gate_grad = hidden_grad * up_act * sigmoid_gate * (1.0 + gate_act * (1.0 - sigmoid_gate))
    up_grad = hidden_grad * gate_act * sigmoid_gate
    both = jnp.concatenate([gate_grad, up_grad], axis=1).astype(jnp.bfloat16)
    normed_grad = lax.dot_general(both, wide_w, contract_cols, preferred_element_type=jnp.float32)
    widened = inputs.astype(jnp.float32)
    inv_rms = lax.rsqrt(jnp.mean(widened * widened, axis=-1, keepdims=True) + EPSILON)
    input_grad = upstream.astype(jnp.float32) + inv_rms * normed_grad
    input_grad = input_grad - widened * inv_rms**3 * jnp.mean(
        normed_grad * widened, axis=-1, keepdims=True
    )
    return input_grad.astype(jnp.bfloat16)


def local_direct(tokens, gate_weight, up_weight, slow_down, prev_outer, route, partner):
    section_count = lax.axis_size("section")
    replica_count = lax.axis_size("replica")
    section_id = lax.axis_index("section")
    replica_id = lax.axis_index("replica")
    gate_w = gate_weight[0, 0]
    up_w = up_weight[0, 0]
    slow_weight = slow_down[0, 0]
    prior_outer = prev_outer[0, 0]
    down_w = slow_weight.astype(jnp.bfloat16)
    idle = jnp.int32(replica_count)

    table = jnp.concatenate([route[:, 0], partner[None]], axis=0)
    lanes = jnp.arange(replica_count, dtype=jnp.int32)[None]
    row = jnp.arange(section_count, dtype=jnp.int32)
    onward = jnp.sum(jnp.where(lanes == replica_id, table, 0), axis=1)
    origin = jnp.sum(jnp.where(table == replica_id, lanes, 0), axis=1)
    other = jnp.where(row + 1 == section_id, origin, onward) + replica_id
    classes = jnp.where(other >= replica_count, other - replica_count, other)
    taking_part = (row == section_id) | (row + 1 == section_id) | (row == section_count - 1)
    choices = jnp.where(taking_part, classes, idle)

    counts = (section_count, replica_count)

    def hop(value, h, way):
        ways = 0 if h % 2 else way
        sets = [hop_pairs(h % 2, k, *counts, ways) for k in range(replica_count)]
        return choose_transfer(value, choices[h], sets)

    mate_sets = [mate_pairs(k, *counts) for k in range(1, replica_count)]
    odd = section_id % 2 == 1
    final = section_id == section_count - 1
    mate_class = (onward[section_count - 1] ^ replica_id) - 1
    side = jnp.sum(jnp.where(lanes[0] == replica_id ^ 1, partner, 0))
    flip_class = (side ^ replica_id ^ 1) - 1

    def flip(held, sections):
        pairs = [
            (s * replica_count + i, s * replica_count + (i ^ 1))
            for s in sections
            for i in range(replica_count)
        ]
        return lax.ppermute(held, AXES, pairs)

    def gossip(held, sections, turned=None):
        here = section_id == sections[0]
        for s in sections[1:]:
            here = here | (section_id == s)

        def step(index, held):
            if turned is None:
                return choose_transfer(held, mate_class, mate_sets)
            held = jnp.where(odd, turned, held)
            return choose_transfer(held, jnp.where(odd, flip_class, mate_class), mate_sets)

        return lax.fori_loop(0, here.astype(jnp.int32), step, held)

    def ordered(*values):
        return lax.optimization_barrier(values)

    wide_w = jnp.concatenate([gate_w, up_w], axis=1)

    def forward(rows):
        output, acts, hidden = joint_forward(rows, wide_w, down_w)
        return output, (rows, acts, hidden)

    def backward(kept, upstream):
        return joint_backward(kept[0], kept[1], upstream, wide_w, down_w)

    pieces = [tokens[0]]
    for s in range(1, section_count):
        pairs = [(s * replica_count + i, i) for i in range(replica_count)]
        pieces.append(lax.ppermute(tokens[0], AXES, pairs))
    inputs = jnp.concatenate(pieces, axis=0)
    slow, prior = down_w, prior_outer
    inputs, slow, prior = ordered(inputs, slow, prior)
    turned_slow = flip(slow, [3])
    turned_prior = flip(prior, [1, 3])
    slow = gossip(slow, [1, 2])
    output, kept_0 = forward(inputs)
    output, slow = ordered(output, slow)
    inputs = hop(output, 0, 1)
    inputs, slow, prior = ordered(inputs, slow, prior)
    prior = gossip(prior, [2])
    slow = gossip(slow, [3], turned_slow)
    inputs, slow = ordered(inputs, slow)
    output, kept_1 = forward(inputs)
    output, slow, prior = ordered(output, slow, prior)
    inputs = hop(output, 1, 1)
    inputs, slow, prior = ordered(inputs, slow, prior)
    prior = gossip(prior, [0, 1, 3], turned_prior)
    inputs, slow, prior = ordered(inputs, slow, prior)
    slow_back = flip(slow, [3])
    prior_back = flip(prior, [1, 3])
    slow = gossip(slow, [0])
    output, kept_2 = forward(inputs)
    output, slow, prior = ordered(output, slow, prior)
    inputs = hop(output, 2, 1)
    output, kept_3 = forward(inputs)
    upstream_3 = (output.astype(jnp.float32) / float(MB * MT)).astype(jnp.bfloat16)
    input_grad = backward(kept_3, upstream_3)
    upstream_2 = hop(input_grad, 2, -1)
    input_grad = backward(kept_2, upstream_2)
    upstream_1 = hop(input_grad, 1, -1)
    input_grad = backward(kept_1, upstream_1)
    input_grad, prior = ordered(input_grad, prior)
    upstream_0 = hop(input_grad, 0, -1)
    slow = jnp.where(final, slow_back, slow)
    prior = jnp.where(odd, prior_back, prior)

    hidden, upstream = kept_0[2], upstream_0
    for s, kept, grad in ((1, kept_1, upstream_1), (2, kept_2, upstream_2), (3, kept_3, upstream_3)):
        hidden = jnp.where(section_id == s, kept[2], hidden)
        upstream = jnp.where(section_id == s, grad, upstream)
    weight_grad = lax.dot_general(
        hidden, upstream, (((0,), (0,)), ((), ())), preferred_element_type=jnp.float32
    )
    average_slow = 0.5 * (slow_weight + slow.astype(jnp.float32))
    average_prev = 0.5 * (prior_outer.astype(jnp.float32) + prior.astype(jnp.float32))
    velocity = MOMENTUM * average_prev + weight_grad
    new_slow = average_slow - OUTER_RATE * (weight_grad + MOMENTUM * velocity)
    return (new_slow[None, None], velocity.astype(jnp.bfloat16)[None, None])


def solution(mesh):
    pair_sets = 4 * mesh.shape["replica"] + mesh.shape["section"]
    paired = mesh.shape["replica"] & (mesh.shape["replica"] - 1) == 0
    direct = paired and mesh.shape["section"] == DIRECT_SECTIONS and pair_sets <= DIRECT_SETS
    local = local_direct if direct else local_exchange
    placed = (
        P("replica", "section", None),
        P("section", "replica", None, None),
        P("section", "replica", None, None),
        P("section", "replica", None, None),
        P("section", "replica", None, None),
        P(),
        P(),
    )
    return jax.shard_map(
        local,
        mesh=mesh,
        in_specs=placed,
        out_specs=(P("section", "replica", None, None), P("section", "replica", None, None)),
        check_vma=False,
    )
```

```python
import jax
import jax.numpy as jnp
from jax import lax
from jax.sharding import PartitionSpec as P

MT = 128
MB = 1


EPSILON = 1e-05
OUTER_RATE = 0.7
MOMENTUM = 0.9
DIRECT_SETS = 36
AXES = ("section", "replica")
DIRECT_SECTIONS = 4


def for_sending(shard):
    return jax.tree.map(lambda a: a.astype(jnp.bfloat16) if a.dtype == jnp.float32 else a, shard)


def passed_along(shard, axis, by):
    length = lax.axis_size(axis)
    pairs = [(i, i + by) for i in range(length) if 0 <= i + by < length]
    return lax.ppermute(shard, axis, pairs)


def section_forward(inputs, gate_w, up_w, down_w):
    widened = inputs.astype(jnp.float32)
    inv_rms = lax.rsqrt(jnp.mean(widened * widened, axis=-1, keepdims=True) + EPSILON)
    normed = (widened * inv_rms).astype(jnp.bfloat16)
    gate_act = jnp.dot(normed, gate_w, preferred_element_type=jnp.float32)
    up_act = jnp.dot(normed, up_w, preferred_element_type=jnp.float32)
    hidden = (jax.nn.silu(gate_act) * up_act).astype(jnp.bfloat16)
    output = (widened + jnp.dot(hidden, down_w, preferred_element_type=jnp.float32)).astype(
        jnp.bfloat16
    )
    return (output, gate_act, up_act, hidden)


def section_backward(inputs, gate_act, up_act, hidden, upstream, gate_w, up_w, down_w):
    contract_rows = (((0,), (0,)), ((), ()))
    contract_cols = (((1,), (1,)), ((), ()))
    grad_part = lax.dot_general(hidden, upstream, contract_rows, preferred_element_type=jnp.float32)
    hidden_grad = lax.dot_general(
        upstream, down_w, contract_cols, preferred_element_type=jnp.float32
    )
    sigmoid_gate = jax.nn.sigmoid(gate_act)
    gate_grad = (
        hidden_grad * up_act * sigmoid_gate * (1.0 + gate_act * (1.0 - sigmoid_gate))
    ).astype(jnp.bfloat16)
    up_grad = (hidden_grad * gate_act * sigmoid_gate).astype(jnp.bfloat16)
    normed_grad = lax.dot_general(
        gate_grad, gate_w, contract_cols, preferred_element_type=jnp.float32
    )
    normed_grad = normed_grad + lax.dot_general(
        up_grad, up_w, contract_cols, preferred_element_type=jnp.float32
    )
    widened = inputs.astype(jnp.float32)
    inv_rms = lax.rsqrt(jnp.mean(widened * widened, axis=-1, keepdims=True) + EPSILON)
    input_grad = upstream.astype(jnp.float32) + inv_rms * normed_grad
    input_grad = input_grad - widened * inv_rms**3 * jnp.mean(
        normed_grad * widened, axis=-1, keepdims=True
    )
    return (grad_part, input_grad.astype(jnp.bfloat16))


def permute_matrix(targets, replica_count):
    return (targets[None, :] == jnp.arange(replica_count, dtype=jnp.int32)[:, None]).astype(
        jnp.bfloat16
    )


def reorder(received, matrix):
    flat_rows = received.reshape(received.shape[0], -1)
    placed = jnp.dot(matrix, flat_rows, preferred_element_type=jnp.float32).astype(jnp.bfloat16)
    return placed.reshape(received.shape)


def route_block(act_block, matrix):
    return lax.all_to_all(
        reorder(
            lax.all_to_all(act_block[None], "replica", split_axis=2, concat_axis=0, tiled=True),
            matrix,
        ),
        "replica",
        split_axis=0,
        concat_axis=2,
        tiled=True,
    )[0]


def partner_copy(slow_weight, prior_outer, partner):
    received = (
        lax.all_to_all(
            slow_weight[None].astype(jnp.bfloat16),
            "replica",
            split_axis=1,
            concat_axis=0,
            tiled=True,
        ).astype(jnp.float32),
        lax.all_to_all(prior_outer[None], "replica", split_axis=1, concat_axis=0, tiled=True),
    )
    mates = lax.all_to_all(
        for_sending(tuple((jnp.take(member, partner, axis=0) for member in received))),
        "replica",
        split_axis=0,
        concat_axis=1,
        tiled=True,
    )
    return (mates[0][0], mates[1][0])


def store_slot(buffer, slot_index, is_live, new_value):
    previous = buffer[slot_index]
    return buffer.at[slot_index].set(jnp.where(is_live, new_value, previous))


def local_exchange(tokens, gate_weight, up_weight, slow_down, prev_outer, route, partner):
    section_count = lax.axis_size("section")
    replica_count = lax.axis_size("replica")
    section_id = lax.axis_index("section")
    gate_w = gate_weight[0, 0]
    up_w = up_weight[0, 0]
    slow_weight = slow_down[0, 0]
    prior_outer = prev_outer[0, 0]
    down_w = slow_weight.astype(jnp.bfloat16)
    feature_count = gate_w.shape[0]
    hidden_units = gate_w.shape[1]
    gathered = lax.all_gather(tokens[0], "section", axis=0, tiled=True).reshape(
        MB, MT, feature_count
    )
    turn_count = MB + section_count - 1
    saved_in = jnp.zeros((MB, MT, feature_count), jnp.bfloat16)
    saved_out = jnp.zeros((MB, MT, feature_count), jnp.bfloat16)
    saved_gate = jnp.zeros((MB, MT, hidden_units), jnp.float32)
    saved_up = jnp.zeros((MB, MT, hidden_units), jnp.float32)
    saved_hidden = jnp.zeros((MB, MT, hidden_units), jnp.bfloat16)
    arriving = jnp.zeros((MT, feature_count), jnp.bfloat16)
    for turn_index in range(turn_count):
        micro_batch = turn_index - section_id
        is_live = (micro_batch >= 0) & (micro_batch < MB)
        slot_index = jnp.clip(micro_batch, 0, MB - 1)
        fresh_rows = gathered[min(turn_index, MB - 1)]
        inputs = jnp.where(section_id == 0, fresh_rows, arriving)
        output, gate_act, up_act, hidden = section_forward(inputs, gate_w, up_w, down_w)
        saved_in = store_slot(saved_in, slot_index, is_live, inputs)
        saved_out = store_slot(saved_out, slot_index, is_live, output)
        saved_gate = store_slot(saved_gate, slot_index, is_live, gate_act)
        saved_up = store_slot(saved_up, slot_index, is_live, up_act)
        saved_hidden = store_slot(saved_hidden, slot_index, is_live, hidden)
        if turn_index < turn_count - 1:
            boundary = jnp.minimum(section_id, section_count - 2)
            matrix = permute_matrix(route[boundary, slot_index], replica_count)
            arriving = passed_along(route_block(output, matrix), "section", 1)
    weight_grad = jnp.zeros((hidden_units, feature_count), jnp.float32)
    arriving = jnp.zeros((MT, feature_count), jnp.bfloat16)
    for turn_index in range(turn_count):
        micro_batch = turn_index - (section_count - 1 - section_id)
        is_live = (micro_batch >= 0) & (micro_batch < MB)
        slot_index = jnp.clip(micro_batch, 0, MB - 1)
        loss_grad = (saved_out[slot_index].astype(jnp.float32) / float(MB * MT)).astype(
            jnp.bfloat16
        )
        upstream = jnp.where(section_id == section_count - 1, loss_grad, arriving)
        grad_part, input_grad = section_backward(
            saved_in[slot_index],
            saved_gate[slot_index],
            saved_up[slot_index],
            saved_hidden[slot_index],
            upstream,
            gate_w,
            up_w,
            down_w,
        )
        weight_grad = weight_grad + jnp.where(is_live, grad_part, 0.0)
        if turn_index < turn_count - 1:
            boundary = jnp.maximum(section_id - 1, 0)
            matrix = permute_matrix(route[boundary, slot_index], replica_count).T
            arriving = passed_along(route_block(input_grad, matrix), "section", -1)
    mate_slow, mate_prior = partner_copy(slow_weight, prior_outer, partner)
    average_slow = 0.5 * (slow_weight + mate_slow)
    average_prev = 0.5 * (prior_outer.astype(jnp.float32) + mate_prior.astype(jnp.float32))
    velocity = MOMENTUM * average_prev + weight_grad
    new_slow = average_slow - OUTER_RATE * (weight_grad + MOMENTUM * velocity)
    return (new_slow[None, None], velocity.astype(jnp.bfloat16)[None, None])


def reflected(k, i, length):
    return (k - i) % length


def hop_pairs(parity, k, section_count, replica_count, way):
    pairs = []
    for h in range(parity, section_count - 1, 2):
        for i in range(replica_count):
            low = h * replica_count + i
            high = (h + 1) * replica_count + reflected(k, i, replica_count)
            if way >= 0:
                pairs.append((low, high))
            if way <= 0:
                pairs.append((high, low))
    return pairs


def mate_pairs(k, section_count, replica_count):
    return [
        (s * replica_count + i, s * replica_count + (i ^ k))
        for s in range(section_count)
        for i in range(replica_count)
    ]


def choose_transfer(value, choice, pair_sets):
    branches = [lambda v, pairs=pairs: lax.ppermute(v, AXES, pairs) for pairs in pair_sets]
    branches.append(lambda v: v)
    return lax.switch(choice, branches, value)


def joint_forward(inputs, wide_w, down_w):
    hidden_units = wide_w.shape[1] // 2
    widened = inputs.astype(jnp.float32)
    inv_rms = lax.rsqrt(jnp.mean(widened * widened, axis=-1, keepdims=True) + EPSILON)
    normed = (widened * inv_rms).astype(jnp.bfloat16)
    acts = jnp.dot(normed, wide_w, preferred_element_type=jnp.float32)
    gate_act, up_act = acts[:, :hidden_units], acts[:, hidden_units:]
    hidden = (jax.nn.silu(gate_act) * up_act).astype(jnp.bfloat16)
    output = (widened + jnp.dot(hidden, down_w, preferred_element_type=jnp.float32)).astype(
        jnp.bfloat16
    )
    return output, acts, hidden


def joint_backward(inputs, acts, upstream, wide_w, down_w):
    contract_cols = (((1,), (1,)), ((), ()))
    hidden_units = wide_w.shape[1] // 2
    gate_act, up_act = acts[:, :hidden_units], acts[:, hidden_units:]
    hidden_grad = lax.dot_general(
        upstream, down_w, contract_cols, preferred_element_type=jnp.float32
    )
    sigmoid_gate = jax.nn.sigmoid(gate_act)
    gate_grad = hidden_grad * up_act * sigmoid_gate * (1.0 + gate_act * (1.0 - sigmoid_gate))
    up_grad = hidden_grad * gate_act * sigmoid_gate
    both = jnp.concatenate([gate_grad, up_grad], axis=1).astype(jnp.bfloat16)
    normed_grad = lax.dot_general(both, wide_w, contract_cols, preferred_element_type=jnp.float32)
    widened = inputs.astype(jnp.float32)
    inv_rms = lax.rsqrt(jnp.mean(widened * widened, axis=-1, keepdims=True) + EPSILON)
    input_grad = upstream.astype(jnp.float32) + inv_rms * normed_grad
    input_grad = input_grad - widened * inv_rms**3 * jnp.mean(
        normed_grad * widened, axis=-1, keepdims=True
    )
    return input_grad.astype(jnp.bfloat16)


def local_direct(tokens, gate_weight, up_weight, slow_down, prev_outer, route, partner):
    section_count = lax.axis_size("section")
    replica_count = lax.axis_size("replica")
    section_id = lax.axis_index("section")
    replica_id = lax.axis_index("replica")
    gate_w = gate_weight[0, 0]
    up_w = up_weight[0, 0]
    slow_weight = slow_down[0, 0]
    prior_outer = prev_outer[0, 0]
    down_w = slow_weight.astype(jnp.bfloat16)
    idle = jnp.int32(replica_count)

    table = jnp.concatenate([route[:, 0], partner[None]], axis=0)
    lanes = jnp.arange(replica_count, dtype=jnp.int32)[None]
    row = jnp.arange(section_count, dtype=jnp.int32)
    onward = jnp.sum(jnp.where(lanes == replica_id, table, 0), axis=1)
    origin = jnp.sum(jnp.where(table == replica_id, lanes, 0), axis=1)
    other = jnp.where(row + 1 == section_id, origin, onward) + replica_id
    classes = jnp.where(other >= replica_count, other - replica_count, other)
    taking_part = (row == section_id) | (row + 1 == section_id) | (row == section_count - 1)
    choices = jnp.where(taking_part, classes, idle)

    counts = (section_count, replica_count)

    def hop(value, h, way):
        ways = 0 if h % 2 else way
        sets = [hop_pairs(h % 2, k, *counts, ways) for k in range(replica_count)]
        return choose_transfer(value, choices[h], sets)

    mate_sets = [mate_pairs(k, *counts) for k in range(1, replica_count)]
    odd = section_id % 2 == 1
    final = section_id == section_count - 1
    mate_class = (onward[section_count - 1] ^ replica_id) - 1
    side = jnp.sum(jnp.where(lanes[0] == replica_id ^ 1, partner, 0))
    flip_class = (side ^ replica_id ^ 1) - 1

    def flip(held, sections):
        pairs = [
            (s * replica_count + i, s * replica_count + (i ^ 1))
            for s in sections
            for i in range(replica_count)
        ]
        return lax.ppermute(held, AXES, pairs)

    def gossip(held, sections, turned=None):
        here = section_id == sections[0]
        for s in sections[1:]:
            here = here | (section_id == s)

        def step(index, held):
            if turned is None:
                return choose_transfer(held, mate_class, mate_sets)
            held = jnp.where(odd, turned, held)
            return choose_transfer(held, jnp.where(odd, flip_class, mate_class), mate_sets)

        return lax.fori_loop(0, here.astype(jnp.int32), step, held)

    def ordered(*values):
        return lax.optimization_barrier(values)

    wide_w = jnp.concatenate([gate_w, up_w], axis=1)

    def forward(rows):
        output, acts, hidden = joint_forward(rows, wide_w, down_w)
        return output, (rows, acts, hidden)

    def backward(kept, upstream):
        return joint_backward(kept[0], kept[1], upstream, wide_w, down_w)

    pieces = [tokens[0]]
    for s in range(1, section_count):
        pairs = [(s * replica_count + i, i) for i in range(replica_count)]
        pieces.append(lax.ppermute(tokens[0], AXES, pairs))
    inputs = jnp.concatenate(pieces, axis=0)
    slow, prior = down_w, prior_outer
    inputs, slow, prior = ordered(inputs, slow, prior)
    turned_slow = flip(slow, [3])
    turned_prior = flip(prior, [1, 3])
    slow = gossip(slow, [1, 2])
    output, kept_0 = forward(inputs)
    output, slow = ordered(output, slow)
    inputs = hop(output, 0, 1)
    inputs, slow, prior = ordered(inputs, slow, prior)
    slow = gossip(slow, [0])
    prior = gossip(prior, [2])
    inputs, slow = ordered(inputs, slow)
    output, kept_1 = forward(inputs)
    output, slow, prior = ordered(output, slow, prior)
    inputs = hop(output, 1, 1)
    inputs, slow, prior = ordered(inputs, slow, prior)
    slow = gossip(slow, [3], turned_slow)
    prior, slow = ordered(prior, slow)
    prior = gossip(prior, [0, 1, 3], turned_prior)
    inputs, slow, prior = ordered(inputs, slow, prior)
    slow_back = flip(slow, [3])
    prior_back = flip(prior, [1, 3])
    def upper_turns(inputs, hidden):
        output, kept_2 = forward(inputs)
        rows = hop(output, 2, 1)
        output, kept_3 = forward(rows)
        upstream_3 = (output.astype(jnp.float32) / float(MB * MT)).astype(jnp.bfloat16)
        upstream_2 = hop(backward(kept_3, upstream_3), 2, -1)
        input_grad = backward(kept_2, upstream_2)
        hidden = jnp.where(final, kept_3[2], kept_2[2])
        return input_grad, hidden, jnp.where(final, upstream_3, upstream_2)

    hidden = jnp.where(section_id == 0, kept_0[2], kept_1[2])
    input_grad, hidden, upstream = lax.cond(
        section_id >= 2, upper_turns, lambda rows, hidden: (rows, hidden, rows), inputs, hidden
    )
    input_grad, prior = ordered(input_grad, prior)
    upstream_1 = hop(input_grad, 1, -1)
    input_grad = backward(kept_1, upstream_1)
    input_grad, prior = ordered(input_grad, prior)
    upstream_0 = hop(input_grad, 0, -1)
    slow = jnp.where(final, slow_back, slow)
    prior = jnp.where(odd, prior_back, prior)

    upstream = jnp.where(section_id == 0, upstream_0, upstream)
    upstream = jnp.where(section_id == 1, upstream_1, upstream)
    weight_grad = lax.dot_general(
        hidden, upstream, (((0,), (0,)), ((), ())), preferred_element_type=jnp.float32
    )
    average_slow = 0.5 * (slow_weight + slow.astype(jnp.float32))
    average_prev = 0.5 * (prior_outer.astype(jnp.float32) + prior.astype(jnp.float32))
    velocity = MOMENTUM * average_prev + weight_grad
    new_slow = average_slow - OUTER_RATE * (weight_grad + MOMENTUM * velocity)
    return (new_slow[None, None], velocity.astype(jnp.bfloat16)[None, None])


def solution(mesh):
    pair_sets = 4 * mesh.shape["replica"] + mesh.shape["section"]
    paired = mesh.shape["replica"] & (mesh.shape["replica"] - 1) == 0
    direct = paired and mesh.shape["section"] == DIRECT_SECTIONS and pair_sets <= DIRECT_SETS
    local = local_direct if direct else local_exchange
    placed = (
        P("replica", "section", None),
        P("section", "replica", None, None),
        P("section", "replica", None, None),
        P("section", "replica", None, None),
        P("section", "replica", None, None),
        P(),
        P(),
    )
    return jax.shard_map(
        local,
        mesh=mesh,
        in_specs=placed,
        out_specs=(P("section", "replica", None, None), P("section", "replica", None, None)),
        check_vma=False,
    )
```
